256 devices in a mesh: pop: 32 (over z_hi, x, core), shard: 8 (over z_lo, y).
Axes of the slice: x: 4, y: 4, z: 8 (z_hi: 4, z_lo: 2; z = z_hi * 2 + z_lo), core: 2. Of those that a mesh axis runs over, the one named last changes fastest.
Arguments:
- hidden: bfloat16 [64, 4096, 4096], P('pop', 'shard'), may hold values from -6 to 6
- norm_scale_vector: float32 [4096], replicated, may hold values from 0.3 to 3
- w_value: bfloat16 [4096, 1024], P('shard'), may hold values from -0.09375 to 0.09375
- model_side_factor: bfloat16 [64, 4, 4096], P('pop'), may hold values from -0.09375 to 0.09375
- value_side_factor: bfloat16 [64, 4, 1024], P('pop'), may hold values from -3 to 3
- target: bfloat16 [64, 4096, 1024], P('pop', 'shard'), may hold values from -6 to 6
- lengths: int32 [64], P('pop'), may hold values from 1 to 4096, 163840 in all
- fitness_ranks: int32 [64], replicated, may hold values from 0 to 63, each once
Outputs:
- losses: float32 [64, 4096], P('pop', 'shard')
- scores: float32 [64], P('pop')
- weight_step: bfloat16 [4096, 1024], P('shard')
The draws below stay inside these ranges and needn't reach their ends.
Inputs may be any that keep to these rules, and one draw needn't show every extreme that they name: Positions t < lengths[m] of member m are live; the lengths of all members sum to 163840, and some member has exactly 4096. `fitness_ranks`: each of 0 to 63 appears once.
All inputs are finite; a program needn't handle non-finite values. No bound on the sum of `lengths` on one device may be relied on, other than what follows from the above.
Results may differ from the reference program's by a relative error of at most 0.0048.
Values may be sent and summed in bfloat16 or wider, within the bound.
A program may use at most 64 MiB of HBM per device.

```python
import math
import jax
import jax.numpy as jnp
import numpy as np
from jax import lax

D = 4096
KV = 1024
RANK = 4
MEMBERS = 64
SEQ = 4096
LIVE = 163840


def block_scale(key, extent, split, least, high):
    def one(dim, shards_of):
        draws = jax.random.uniform(jax.random.fold_in(jax.random.fold_in(key, 6), dim), (shards_of,), jnp.float32, least / len(split), high / len(split))
        return jnp.repeat(jnp.exp(draws), extent[dim] // shards_of).reshape((-1,) + (1,) * (len(extent) - dim - 1))

    level = one(*split[0])
    for cut in split[1:]:
        level = level * one(*cut)
    return level


def split_up(count, total, most, skew):
    portions = [(1 << 20) // math.isqrt(standing ** skew) + 1 for standing in range(2, count + 1)]
    spare, holding = total - most - (count - 1), [1] * (count - 1)
    while spare > 0:
        candidates = [i for i in range(count - 1) if holding[i] < most]
        whole, budget = sum([portions[i] for i in candidates]), spare
        for i in candidates:
            extra = min(most - holding[i], max(1, budget * portions[i] // whole), spare)
            holding[i] = holding[i] + extra
            spare = spare - extra
    return np.array([most] + holding)


def uneven(own_key, amount, total, most, slope):
    if amount == 2:
        one = jax.random.randint(own_key, (), max(1, total - most), min(most, total - 1) + 1)
        return jnp.stack([one, total - one])
    tallies = jnp.asarray(split_up(amount, total, most, slope), jnp.int32)
    pairs = (amount - 1) // 2
    giver, receiver = tallies[1:1 + 2 * pairs:2], tallies[2:2 + 2 * pairs:2]
    margin = jnp.minimum(giver - 1, most - receiver)
    shifted = jax.random.randint(jax.random.fold_in(own_key, 1), (pairs,), 0, 1 << 20) % (margin + 1)
    tallies = tallies.at[1:1 + 2 * pairs:2].set(giver - shifted).at[2:2 + 2 * pairs:2].set(receiver + shifted)
    return tallies[jax.random.permutation(jax.random.fold_in(own_key, 2), amount)]


def normal_values(key, extent, scale, bound, split=(), kind=jnp.bfloat16):
    drawn = scale * jax.random.normal(key, extent, jnp.float32)
    if split:
        drawn = drawn * block_scale(key, extent, split, -0.22, 0.18)
    return jnp.clip(drawn, -bound, bound).astype(kind)


def setup_inputs(seed: int = 0) -> dict:
    keys = jax.random.split(jax.random.key(seed), 9)
    return {
        "hidden": normal_values(keys[0], (MEMBERS, SEQ, D), 1.0, 6.0, ((0, 32), (1, 8))),
        "norm_scale_vector": jnp.clip(jnp.exp(jax.random.uniform(keys[1], (D,), jnp.float32, math.log(0.3), math.log(3.0))), 0.3, 3.0),
        "w_value": normal_values(keys[2], (D, KV), D ** -0.5, 0.09375, ((0, 8),)),
        "model_side_factor": normal_values(keys[3], (MEMBERS, RANK, D), D ** -0.5, 0.09375, ((0, 32),)),
        "value_side_factor": normal_values(keys[4], (MEMBERS, RANK, KV), RANK ** -0.5, 3.0, ((0, 32),)),
        "target": normal_values(keys[5], (MEMBERS, SEQ, KV), 1.0, 6.0, ((0, 32), (1, 8))),
        "lengths": uneven(keys[6], MEMBERS, LIVE, SEQ, 2).astype(jnp.int32),
        "fitness_ranks": jax.random.permutation(keys[7], MEMBERS).astype(jnp.int32),
    }


def reference(hidden, norm_scale_vector, w_value, model_side_factor, value_side_factor, target, lengths, fitness_ranks):

    def one_member(packed):
        states, left_one, right_one, teacher, length_one = packed
        widened = states.astype(jnp.float32)
        inverse = lax.rsqrt(lax.optimization_barrier(jnp.mean(widened * widened, axis=-1, keepdims=True)) + 1e-05)
        normalized_input = (widened * inverse * norm_scale_vector).astype(jnp.bfloat16)
        projected = jnp.dot(normalized_input, w_value, preferred_element_type=jnp.float32)
        reduced_output = jnp.dot(normalized_input, left_one.T, preferred_element_type=jnp.float32).astype(jnp.bfloat16)
        lateral_product = jnp.dot(reduced_output, right_one, preferred_element_type=jnp.float32)
        values = projected + 0.1 * lateral_product
        errors = values - teacher.astype(jnp.float32)
        squared = lax.optimization_barrier(jnp.mean(errors * errors, axis=-1))
        position = jnp.arange(states.shape[0], dtype=jnp.int32)
        masked = jnp.where(position < length_one, squared, 0.0)
        return (masked, jnp.sum(masked) / length_one.astype(jnp.float32))
    losses, scores = lax.map(one_member, (hidden, model_side_factor, value_side_factor, target, lengths))
    fitness = fitness_ranks.astype(jnp.float32) / (MEMBERS - 1) - 0.5
    scaled_left = (model_side_factor.astype(jnp.float32) * fitness[:, None, None]).astype(jnp.bfloat16)
    summed_step = jnp.einsum('mri,mrj->ij', scaled_left.astype(jnp.float32), value_side_factor.astype(jnp.float32), precision=lax.Precision.HIGHEST)
    weight_step = (summed_step * (math.sqrt(D) / (0.1 * MEMBERS))).astype(jnp.bfloat16)
    return (losses, scores, weight_step)
```

```python
import math

import jax
import jax.numpy as jnp
from jax import lax
from jax.sharding import PartitionSpec as P

noise_scale = 0.1
epsilon = 1e-05


def on_device(
    hidden,
    norm_scale_vector,
    w_value,
    model_side_factor,
    value_side_factor,
    target,
    lengths,
    fitness_ranks,
):
    members, span_here, width = hidden.shape
    share, outputs = w_value.shape
    everyone = fitness_ranks.shape[0]
    widened = hidden.astype(jnp.float32)
    inverse = lax.rsqrt(jnp.mean(widened * widened, axis=-1, keepdims=True) + epsilon)
    normalized_input = (widened * inverse * norm_scale_vector).astype(jnp.bfloat16)
    flattened = normalized_input.reshape(members * span_here, width)
    projected = jnp.dot(
        flattened,
        lax.all_gather(w_value, "shard", axis=0, tiled=True),
        preferred_element_type=jnp.float32,
    )
    reduced_output = jnp.einsum(
        "uch,ufh->ucf", normalized_input, model_side_factor, preferred_element_type=jnp.float32
    ).astype(jnp.bfloat16)
    lateral_product = jnp.einsum(
        "nfw,nwx->nfx", reduced_output, value_side_factor, preferred_element_type=jnp.float32
    )
    values = projected.reshape(members, span_here, outputs) + noise_scale * lateral_product
    errors = values - target.astype(jnp.float32)
    squared = jnp.mean(errors * errors, axis=-1)
    first_position = lax.axis_index("shard") * span_here
    position = first_position + lax.broadcasted_iota(jnp.int32, (members, span_here), 1)
    losses = jnp.where(position < lengths[:, None], squared, 0.0)
    totals = lax.psum(jnp.sum(losses, axis=1), "shard")
    scores = totals / lengths.astype(jnp.float32)
    column_start = lax.axis_index("shard") * share
    left_rows = lax.dynamic_slice_in_dim(model_side_factor, column_start, share, 2)
    step_factor = math.sqrt(width) / (noise_scale * everyone)
    own_ranks = lax.dynamic_slice_in_dim(fitness_ranks, lax.axis_index("pop") * members, members, 0)
    own_fitness = own_ranks.astype(jnp.float32) / (everyone - 1) - 0.5
    scaled_left = (left_rows.astype(jnp.float32) * own_fitness[:, None, None]).astype(jnp.bfloat16)
    pack = jnp.concatenate([scaled_left, value_side_factor], axis=2)
    pack = pack.reshape(pack.shape[0] * pack.shape[1], pack.shape[2])
    everything = lax.all_gather(pack, "pop", axis=0, tiled=True)
    summed_step = lax.dot_general(
        everything[:, :share],
        everything[:, share:],
        (((0,), (0,)), ((), ())),
        preferred_element_type=jnp.float32,
    )
    weight_step = (summed_step * step_factor).astype(jnp.bfloat16)
    return (losses, scores, weight_step)


def solution(mesh):
    placed = (
        P("pop", "shard", None),
        P(),
        P("shard", None),
        P("pop", None, None),
        P("pop", None, None),
        P("pop", "shard", None),
        P("pop"),
        P(),
    )
    return jax.shard_map(
        on_device,
        mesh=mesh,
        in_specs=placed,
        out_specs=(P("pop", "shard"), P("pop"), P("shard", None)),
        check_vma=False,
    )
```

```python
import math

import jax
import jax.numpy as jnp
from jax import lax
from jax.experimental import pallas as pl
from jax.experimental.pallas import tpu as pltpu
from jax.sharding import PartitionSpec as P

noise_scale = 0.1
epsilon = 1e-05
MESH = pl.DeviceIdType.MESH
NX, NY, NZH, NZL, NC = 4, 4, 4, 2, 2
SHARDS = NZL * NY
POP = NZH * NX * NC


def kernel(
    hidden, gain, weights, left, right, left_in, right_in, target, lengths, ranks,
    losses, scores, step,
    hbuf, nbuf, wbuf, acc, tbuf, abuf, bbuf, fleft, fright, wide_left, wide_right, mine, sums,
    load_sem, send_w, recv_w, send_f, recv_f, send_s, recv_s,
):
    members, span, width = hidden.shape
    share, outputs = weights.shape
    half, quarter = share // 2, share // 4
    pop, shard = lax.axis_index("pop"), lax.axis_index("shard")
    core = lax.rem(pop, NC)
    x = lax.rem(pop // NC, NX)
    zh = pop // (NC * NX)
    zl, y = shard // NY, lax.rem(shard, NY)

    def device(x_, zh_, core_, zl_, y_):
        return (zh_ * (NX * NC) + x_ * NC + core_, zl_ * NY + y_)

    up, down, across = lax.rem(y + 1, NY), lax.rem(y + 3, NY), lax.rem(y + 2, NY)
    other = 1 - zl
    partner = device(x, zh, 1 - core, zl, y)
    y_next, y_prev = device(x, zh, core, zl, up), device(x, zh, core, zl, down)
    z_next = device(x, lax.rem(zh + zl, NZH), core, other, y)
    z_prev = device(x, lax.rem(zh + NZH - other, NZH), core, other, y)
    z_pop = jnp.where(core == 0, z_next[0], z_prev[0])
    z_to = (z_pop, z_next[1])
    z_peers = [device(x, lax.rem(zh + d, NZH), core, zl, y) for d in (1, 2, 3)]
    x_peers = [device(lax.rem(x + d, NX), zh, core, zl, y) for d in (1, 2, 3)]
    shard_peers = [(pop, lax.rem(shard + d, SHARDS)) for d in range(1, SHARDS)]

    own, low_, high, far = zl * NY + y, zl * NY + down, zl * NY + up, zl * NY + across
    own2, low2, high2, far2 = (other * NY + v for v in (y, down, up, across))

    loads = []
    rows = 128
    chunks = members * span // rows
    for j in range(chunks):
        m, q = divmod(j, span // rows)
        loads.append(pltpu.make_async_copy(
            hidden.at[m, pl.ds(q * rows, rows)], hbuf.at[pl.ds(j * rows, rows)], load_sem.at[j]))
    own_load = pltpu.make_async_copy(weights, wbuf.at[own], load_sem.at[chunks])
    slot = core * (NX * NZH) + x * NZH + zh
    columns = pl.ds(pl.multiple_of(shard * share, share), share)
    fl_load = pltpu.make_async_copy(left.at[:, :, columns], fleft.at[slot], load_sem.at[chunks + 1])
    fr_load = pltpu.make_async_copy(right, fright.at[slot], load_sem.at[chunks + 2])
    t_loads = [pltpu.make_async_copy(target.at[m], tbuf.at[pl.ds(m * span, span)],
                                     load_sem.at[chunks + 3 + m]) for m in range(members)]
    for cp in loads + [own_load, fl_load, fr_load] + t_loads:
        cp.start()

    barrier = pltpu.get_barrier_semaphore()
    everyone = [partner, z_next, z_prev] + z_peers + x_peers + shard_peers
    for peer in everyone:
        pl.semaphore_signal(barrier, inc=1, device_id=peer, device_id_type=MESH)
    pl.semaphore_wait(barrier, len(everyone))

    def w_copy(i, src, dst, to):
        return pltpu.make_async_remote_copy(
            src_ref=src, dst_ref=dst, send_sem=send_w.at[i], recv_sem=recv_w.at[i],
            device_id=to, device_id_type=MESH)

    def f_copy(i, src, dst, to):
        return pltpu.make_async_remote_copy(
            src_ref=src, dst_ref=dst, send_sem=send_f.at[i], recv_sem=recv_f.at[i],
            device_id=to, device_id_type=MESH)

    def at(sub):
        return pl.ds(pl.multiple_of(core * half + sub * quarter, quarter), quarter)

    def piece(b, sub):
        return wbuf.at[b, at(sub)]

    def half_of(b, c):
        return wbuf.at[b, pl.ds(pl.multiple_of(c * half, half), half)]

    sent, arrive = {}, {}

    def plan(i, src, dst, landing, to):
        sent[i] = w_copy(i, src, dst, to)
        arrive[i] = w_copy(i, landing, landing, to)

    for i, sub in ((0, 0), (1, 1)):
        plan(i, weights.at[at(sub)], piece(own, sub), piece(low_, sub), y_next)
    plan(2, piece(low_, 0), piece(low_, 0), piece(far, 0), y_next)
    for i, sub in ((3, 1), (4, 0)):
        plan(i, weights.at[at(sub)], piece(own, sub), piece(high, sub), y_prev)
    plan(5, piece(high, 1), piece(high, 1), piece(far, 1), y_prev)
    for i, sub in ((6, 0), (7, 1)):
        plan(i, weights.at[at(sub)], piece(own, sub), piece(own2, sub), z_to)
    for i, b, b2, sub in ((8, low_, low2, 0), (9, high, high2, 1), (10, low_, low2, 1),
                          (11, high, high2, 0), (12, far, far2, 0), (13, far, far2, 1)):
        plan(i, piece(b, sub), piece(b, sub), piece(b2, sub), z_to)
    for i, b in ((14, low_), (15, high), (16, own2), (17, far), (18, low2), (19, high2), (20, far2)):
        plan(i, half_of(b, core), half_of(b, core), half_of(b, 1 - core), partner)

    f_sent = []

    def f_start(i, src, dst, to):
        cp = f_copy(i, src, dst, to)
        cp.start()
        f_sent.append(cp)

    for d in range(3):
        f_start(2 * d, left.at[:, :, columns], fleft.at[slot], z_peers[d])
        f_start(2 * d + 1, right, fright.at[slot], z_peers[d])
    for i in (0, 3, 6, 1, 4, 7):
        sent[i].start()

    for m in range(members):
        pad = jnp.zeros((12, width), jnp.float32)
        a = jnp.concatenate([left_in[m].astype(jnp.float32), pad], axis=0).astype(jnp.bfloat16)
        for b in range(SHARDS):
            abuf[m, b] = a[:, b * share:(b + 1) * share]
        pad = jnp.zeros((12, outputs), jnp.float32)
        bbuf[m] = jnp.concatenate([right_in[m].astype(jnp.float32), pad], axis=0).astype(jnp.bfloat16)

    tile = 16
    for j in range(chunks):
        loads[j].wait()

        def norm(t, carry, j=j):
            r = pl.ds(pl.multiple_of(j * rows + t * tile, tile), tile)
            total = jnp.zeros((tile, share), jnp.float32)
            for b in range(SHARDS):
                v = hbuf[r, b * share:(b + 1) * share].astype(jnp.float32)
                total = total + v * v
            inverse = lax.rsqrt(jnp.sum(total, axis=-1, keepdims=True) / width + epsilon)
            for b in range(SHARDS):
                cols = slice(b * share, (b + 1) * share)
                v = hbuf[r, cols].astype(jnp.float32)
                nbuf[b, r] = (v * inverse * gain[:, cols]).astype(jnp.bfloat16)
            return carry

        lax.fori_loop(0, rows // tile, norm, 0)

    arrive[0].wait_recv()
    sent[2].start()
    sent[8].start()
    arrive[3].wait_recv()
    sent[5].start()
    sent[9].start()

    def f_wait(i, dst):
        f_copy(i, dst, dst, partner).wait_recv()

    for d in range(3):
        back = core * (NX * NZH) + x * NZH + lax.rem(zh + NZH - d - 1, NZH)
        f_wait(2 * d, fleft.at[back])
        f_wait(2 * d + 1, fright.at[back])
    fl_load.wait()
    fr_load.wait()
    group = pl.ds(core * (NX * NZH) + x * NZH, NZH)
    for d in range(3):
        f_start(6 + 2 * d, fleft.at[group], fleft.at[group], x_peers[d])
        f_start(7 + 2 * d, fright.at[group], fright.at[group], x_peers[d])

    for m in range(members):
        r = pl.ds(m * span, span)
        low = jnp.zeros((span, 16), jnp.float32)
        for b in range(SHARDS):
            low = low + lax.dot_general(
                nbuf[b, r], abuf[m, b], (((1,), (1,)), ((), ())), preferred_element_type=jnp.float32)
        low = low.astype(jnp.bfloat16)
        for n in range(0, outputs, 256):
            acc[r, n:n + 256] = noise_scale * jnp.dot(
                low, bbuf[m, :, n:n + 256], preferred_element_type=jnp.float32)

    def multiply(b):
        def body(t, carry):
            c = pl.ds(pl.multiple_of(t * 256, 256), 256)
            acc[:, c] += jnp.dot(nbuf[b], wbuf[b, :, c], preferred_element_type=jnp.float32)
            return carry

        lax.fori_loop(0, outputs // 256, body, 0)

    own_load.wait()
    multiply(own)

    for i in (6, 7):
        arrive[i].wait_recv()
    sent[16].start()
    arrive[1].wait_recv()
    sent[10].start()
    sent[14].start()
    arrive[4].wait_recv()
    sent[11].start()
    sent[15].start()

    for d in range(3):
        g = pl.ds(core * (NX * NZH) + lax.rem(x + NX - d - 1, NX) * NZH, NZH)
        f_wait(6 + 2 * d, fleft.at[g])
        f_wait(7 + 2 * d, fright.at[g])
    mine_f = pl.ds(core * (NX * NZH), NX * NZH)
    f_start(12, fleft.at[mine_f], fleft.at[mine_f], partner)
    f_start(13, fright.at[mine_f], fright.at[mine_f], partner)

    arrive[16].wait_recv()
    multiply(own2)
    arrive[14].wait_recv()
    multiply(low_)
    arrive[2].wait_recv()
    sent[12].start()
    arrive[5].wait_recv()
    sent[13].start()
    sent[17].start()
    arrive[15].wait_recv()
    multiply(high)

    theirs = pl.ds((1 - core) * (NX * NZH), NX * NZH)
    f_wait(12, fleft.at[theirs])
    f_wait(13, fright.at[theirs])
    for k in range(POP):
        c_, rest = divmod(k, NX * NZH)
        x_, zh_ = divmod(rest, NZH)
        first = (zh_ * (NX * NC) + x_ * NC + c_) * members
        for m in range(members):
            r = slice((k * members + m) * 4, (k * members + m) * 4 + 4)
            rank = jnp.full((4, share), ranks[first + m], jnp.int32).astype(jnp.float32)
            fitness = rank / (POP * members - 1) - 0.5
            wide_left[r, :] = fleft[k, m].astype(jnp.float32) * fitness
            wide_right[r, :] = fright[k, m].astype(jnp.float32)
    step_factor = math.sqrt(width) / (noise_scale * POP * members)
    turned = wide_left[...].T.astype(jnp.bfloat16)
    for n in range(0, outputs, 256):
        product = jnp.dot(turned, wide_right[:, n:n + 256].astype(jnp.bfloat16),
                          preferred_element_type=jnp.float32)
        step[:, n:n + 256] = (product * step_factor).astype(jnp.bfloat16)

    arrive[8].wait_recv()
    arrive[10].wait_recv()
    sent[18].start()
    arrive[17].wait_recv()
    multiply(far)
    arrive[9].wait_recv()
    arrive[11].wait_recv()
    sent[19].start()
    arrive[18].wait_recv()
    multiply(low2)
    arrive[12].wait_recv()
    arrive[13].wait_recv()
    sent[20].start()
    arrive[19].wait_recv()
    multiply(high2)
    arrive[20].wait_recv()
    multiply(far2)

    for cp in t_loads:
        cp.wait()
    lanes = lax.broadcasted_iota(jnp.int32, (1, rows), 1)
    partial = []
    for m in range(members):
        running = jnp.zeros((1, rows), jnp.float32)
        for q in range(span // rows):
            r = slice(m * span + q * rows, m * span + (q + 1) * rows)
            part = jnp.zeros((rows, 128), jnp.float32)
            for g in range(0, outputs, 128):
                e = acc[r, g:g + 128] - tbuf[r, g:g + 128].astype(jnp.float32)
                part = part + e * e
            row = jnp.sum(part.T, axis=0, keepdims=True) / outputs
            position = shard * span + q * rows + lanes
            row = jnp.where(position < lengths[m], row, 0.0)
            losses[m:m + 1, q * rows:(q + 1) * rows] = row
            running = running + row
        partial.append(jnp.sum(running, axis=1, keepdims=True))
    which = lax.broadcasted_iota(jnp.int32, (8, 128), 0)
    mine[...] = jnp.where(which == 0, partial[0], partial[1])

    s_sent = []
    for d, peer in enumerate(shard_peers):
        cp = pltpu.make_async_remote_copy(
            src_ref=mine, dst_ref=sums.at[d], send_sem=send_s.at[d], recv_sem=recv_s.at[d],
            device_id=peer, device_id_type=MESH)
        cp.start()
        s_sent.append(cp)
    for i in range(21):
        sent[i].wait_send()
    for cp in f_sent:
        cp.wait_send()
    for cp in s_sent:
        cp.wait()
    whole = jnp.zeros((8, 128), jnp.float32)
    for s in range(SHARDS):
        term = mine[...]
        for d in range(SHARDS - 1):
            term = jnp.where(lax.rem(shard + SHARDS - d - 1, SHARDS) == s, sums[d], term)
        whole = whole + term
    for m in range(members):
        count = jnp.full((8, 128), lengths[m], jnp.int32).astype(jnp.float32)
        scores[m] = (whole / count)[m, 0]


def on_device(hidden, gain, weights, left, right, target, lengths, ranks):
    members, span, width = hidden.shape
    share, outputs = weights.shape
    rank = left.shape[1]
    tokens = members * span
    bf, f32 = jnp.bfloat16, jnp.float32
    hbm = pl.BlockSpec(memory_space=pl.ANY)
    vmem = pl.BlockSpec(memory_space=pltpu.VMEM)
    smem = pl.BlockSpec(memory_space=pltpu.SMEM)
    dma = pltpu.SemaphoreType.DMA
    return tuple(pl.pallas_call(
        kernel,
        out_shape=(
            jax.ShapeDtypeStruct((members, span), f32),
            jax.ShapeDtypeStruct((members,), f32),
            jax.ShapeDtypeStruct((share, outputs), bf),
        ),
        in_specs=[hbm, vmem, hbm, hbm, hbm, vmem, vmem, hbm, smem, smem],
        out_specs=(vmem, smem, vmem),
        scratch_shapes=[
            pltpu.VMEM((tokens, width), bf),
            pltpu.VMEM((SHARDS, tokens, share), bf),
            pltpu.VMEM((SHARDS, share, outputs), bf),
            pltpu.VMEM((tokens, outputs), f32),
            pltpu.VMEM((tokens, outputs), bf),
            pltpu.VMEM((members, SHARDS, 16, share), bf),
            pltpu.VMEM((members, 16, outputs), bf),
            pltpu.VMEM((POP, members, rank, share), bf),
            pltpu.VMEM((POP, members, rank, outputs), bf),
            pltpu.VMEM((POP * members * rank, share), f32),
            pltpu.VMEM((POP * members * rank, outputs), f32),
            pltpu.VMEM((8, 128), f32),
            pltpu.VMEM((SHARDS - 1, 8, 128), f32),
            dma((tokens // 128 + 3 + members,)),
            dma((21,)), dma((21,)), dma((14,)), dma((14,)), dma((7,)), dma((7,)),
        ],
        compiler_params=pltpu.CompilerParams(
            collective_id=0, has_side_effects=True, vmem_limit_bytes=56 * 1024 * 1024),
    )(hidden, gain.reshape(1, width), weights, left, right, left, right, target, lengths, ranks))


def solution(mesh):
    placed = (
        P("pop", "shard", None),
        P(),
        P("shard", None),
        P("pop", None, None),
        P("pop", None, None),
        P("pop", "shard", None),
        P("pop"),
        P(),
    )
    return jax.shard_map(
        on_device,
        mesh=mesh,
        in_specs=placed,
        out_specs=(P("pop", "shard"), P("pop"), P("shard", None)),
        check_vma=False,
    )
```

```python
import math

import jax
import jax.numpy as jnp
from jax import lax
from jax.experimental import pallas as pl
from jax.experimental.pallas import tpu as pltpu
from jax.sharding import PartitionSpec as P

noise_scale = 0.1
epsilon = 1e-05
MESH = pl.DeviceIdType.MESH
NX, NY, NZH, NZL, NC = 4, 4, 4, 2, 2
SHARDS = NZL * NY
POP = NZH * NX * NC


def kernel(
    hidden, gain, weights, left, right, left_in, right_in, target, lengths, ranks,
    losses, scores, step,
    hbuf, nbuf, wbuf, acc, tbuf, abuf, bbuf, fleft, fright, wide_left, wide_right, mine, sums,
    load_sem, send_w, recv_w, send_f, recv_f, send_s, recv_s,
):
    members, span, width = hidden.shape
    share, outputs = weights.shape
    half, quarter = share // 2, share // 4
    pop, shard = lax.axis_index("pop"), lax.axis_index("shard")
    core = lax.rem(pop, NC)
    x = lax.rem(pop // NC, NX)
    zh = pop // (NC * NX)
    zl, y = shard // NY, lax.rem(shard, NY)

    def device(x_, zh_, core_, zl_, y_):
        return (zh_ * (NX * NC) + x_ * NC + core_, zl_ * NY + y_)

    up, down, across = lax.rem(y + 1, NY), lax.rem(y + 3, NY), lax.rem(y + 2, NY)
    other = 1 - zl
    partner = device(x, zh, 1 - core, zl, y)
    y_next, y_prev = device(x, zh, core, zl, up), device(x, zh, core, zl, down)
    z_next = device(x, lax.rem(zh + zl, NZH), core, other, y)
    z_prev = device(x, lax.rem(zh + NZH - other, NZH), core, other, y)
    z_pop = jnp.where(core == 0, z_next[0], z_prev[0])
    z_to = (z_pop, z_next[1])
    z_peers = [device(x, lax.rem(zh + d, NZH), core, zl, y) for d in (1, 2, 3)]
    x_peers = [device(lax.rem(x + d, NX), zh, core, zl, y) for d in (1, 2, 3)]
    shard_peers = [(pop, lax.rem(shard + d, SHARDS)) for d in range(1, SHARDS)]

    own, low_, high, far = zl * NY + y, zl * NY + down, zl * NY + up, zl * NY + across
    own2, low2, high2, far2 = (other * NY + v for v in (y, down, up, across))

    loads = []
    rows = 128
    chunks = members * span // rows
    for j in range(chunks):
        m, q = divmod(j, span // rows)
        loads.append(pltpu.make_async_copy(
            hidden.at[m, pl.ds(q * rows, rows)], hbuf.at[pl.ds(j * rows, rows)], load_sem.at[j]))
    own_load = pltpu.make_async_copy(weights, wbuf.at[own], load_sem.at[chunks])
    slot = core * (NX * NZH) + x * NZH + zh
    columns = pl.ds(pl.multiple_of(shard * share, share), share)
    fl_load = pltpu.make_async_copy(left.at[:, :, columns], fleft.at[slot], load_sem.at[chunks + 1])
    fr_load = pltpu.make_async_copy(right, fright.at[slot], load_sem.at[chunks + 2])
    t_loads = [pltpu.make_async_copy(target.at[m], tbuf.at[pl.ds(m * span, span)],
                                     load_sem.at[chunks + 3 + m]) for m in range(members)]
    for cp in loads + [own_load, fl_load, fr_load] + t_loads:
        cp.start()

    barrier = pltpu.get_barrier_semaphore()
    everyone = [partner, z_next, z_prev] + z_peers + x_peers + shard_peers
    for peer in everyone:
        pl.semaphore_signal(barrier, inc=1, device_id=peer, device_id_type=MESH)
    for m in range(members):
        pad = jnp.zeros((12, width), jnp.float32)
        a = jnp.concatenate([left_in[m].astype(jnp.float32), pad], axis=0).astype(jnp.bfloat16)
        for b in range(SHARDS):
            abuf[m, b] = a[:, b * share:(b + 1) * share]
        pad = jnp.zeros((12, outputs), jnp.float32)
        bbuf[m] = jnp.concatenate([right_in[m].astype(jnp.float32), pad], axis=0).astype(jnp.bfloat16)
    pl.semaphore_wait(barrier, len(everyone))

    def w_copy(i, src, dst, to):
        return pltpu.make_async_remote_copy(
            src_ref=src, dst_ref=dst, send_sem=send_w.at[i], recv_sem=recv_w.at[i],
            device_id=to, device_id_type=MESH)

    def f_copy(i, src, dst, to):
        return pltpu.make_async_remote_copy(
            src_ref=src, dst_ref=dst, send_sem=send_f.at[i], recv_sem=recv_f.at[i],
            device_id=to, device_id_type=MESH)

    def at(sub):
        return pl.ds(pl.multiple_of(core * half + sub * quarter, quarter), quarter)

    def piece(b, sub):
        return wbuf.at[b, at(sub)]

    def half_of(b, c):
        return wbuf.at[b, pl.ds(pl.multiple_of(c * half, half), half)]

    sent, arrive = {}, {}

    def plan(i, src, dst, landing, to):
        sent[i] = w_copy(i, src, dst, to)
        arrive[i] = w_copy(i, landing, landing, to)

    for i, sub in ((0, 0), (1, 1)):
        plan(i, weights.at[at(sub)], piece(own, sub), piece(low_, sub), y_next)
    plan(2, piece(low_, 0), piece(low_, 0), piece(far, 0), y_next)
    for i, sub in ((3, 1), (4, 0)):
        plan(i, weights.at[at(sub)], piece(own, sub), piece(high, sub), y_prev)
    plan(5, piece(high, 1), piece(high, 1), piece(far, 1), y_prev)
    for i, sub in ((6, 0), (7, 1)):
        plan(i, weights.at[at(sub)], piece(own, sub), piece(own2, sub), z_to)
    for i, b, b2, sub in ((8, low_, low2, 0), (9, high, high2, 1), (10, low_, low2, 1),
                          (11, high, high2, 0), (12, far, far2, 0), (13, far, far2, 1)):
        plan(i, piece(b, sub), piece(b, sub), piece(b2, sub), z_to)
    for i, b in ((14, low_), (15, high), (16, own2), (17, far), (18, low2), (19, high2), (20, far2)):
        plan(i, half_of(b, core), half_of(b, core), half_of(b, 1 - core), partner)

    f_sent = []

    def f_start(i, src, dst, to):
        cp = f_copy(i, src, dst, to)
        cp.start()
        f_sent.append(cp)

    for d in range(3):
        f_start(2 * d, left.at[:, :, columns], fleft.at[slot], z_peers[d])
        f_start(2 * d + 1, right, fright.at[slot], z_peers[d])
    for i in (0, 3, 6, 1, 4, 7):
        sent[i].start()

    tile = 16
    for j in range(chunks):
        loads[j].wait()

        def norm(t, carry, j=j):
            r = pl.ds(pl.multiple_of(j * rows + t * tile, tile), tile)
            total = jnp.zeros((tile, share), jnp.float32)
            for b in range(SHARDS):
                v = hbuf[r, b * share:(b + 1) * share].astype(jnp.float32)
                total = total + v * v
            inverse = lax.rsqrt(jnp.sum(total, axis=-1, keepdims=True) / width + epsilon)
            for b in range(SHARDS):
                cols = slice(b * share, (b + 1) * share)
                v = hbuf[r, cols].astype(jnp.float32)
                nbuf[b, r] = (v * inverse * gain[:, cols]).astype(jnp.bfloat16)
            return carry

        lax.fori_loop(0, rows // tile, norm, 0)

    arrive[0].wait_recv()
    sent[2].start()
    sent[8].start()
    arrive[3].wait_recv()
    sent[5].start()
    sent[9].start()

    def f_wait(i, dst):
        f_copy(i, dst, dst, partner).wait_recv()

    for m in range(members):
        r = pl.ds(m * span, span)
        low = jnp.zeros((span, 16), jnp.float32)
        for b in range(SHARDS):
            low = low + lax.dot_general(
                nbuf[b, r], abuf[m, b], (((1,), (1,)), ((), ())), preferred_element_type=jnp.float32)
        low = low.astype(jnp.bfloat16)
        for n in range(0, outputs, 256):
            acc[r, n:n + 256] = noise_scale * jnp.dot(
                low, bbuf[m, :, n:n + 256], preferred_element_type=jnp.float32)

    def multiply(b):
        def body(t, carry):
            c = pl.ds(pl.multiple_of(t * 256, 256), 256)
            acc[:, c] += jnp.dot(nbuf[b], wbuf[b, :, c], preferred_element_type=jnp.float32)
            return carry

        lax.fori_loop(0, outputs // 256, body, 0)

    own_load.wait()
    multiply(own)

    for d in range(3):
        back = core * (NX * NZH) + x * NZH + lax.rem(zh + NZH - d - 1, NZH)
        f_wait(2 * d, fleft.at[back])
        f_wait(2 * d + 1, fright.at[back])
    fl_load.wait()
    fr_load.wait()
    group = pl.ds(core * (NX * NZH) + x * NZH, NZH)
    for d in range(3):
        f_start(6 + 2 * d, fleft.at[group], fleft.at[group], x_peers[d])
        f_start(7 + 2 * d, fright.at[group], fright.at[group], x_peers[d])


    for i in (6, 7):
        arrive[i].wait_recv()
    sent[16].start()
    arrive[1].wait_recv()
    sent[10].start()
    sent[14].start()
    arrive[4].wait_recv()
    sent[11].start()
    sent[15].start()

    arrive[16].wait_recv()
    multiply(own2)
    arrive[14].wait_recv()
    multiply(low_)
    arrive[2].wait_recv()
    sent[12].start()
    arrive[5].wait_recv()
    sent[13].start()
    sent[17].start()
    arrive[15].wait_recv()
    multiply(high)

    for d in range(3):
        g = pl.ds(core * (NX * NZH) + lax.rem(x + NX - d - 1, NX) * NZH, NZH)
        f_wait(6 + 2 * d, fleft.at[g])
        f_wait(7 + 2 * d, fright.at[g])
    mine_f = pl.ds(core * (NX * NZH), NX * NZH)
    f_start(12, fleft.at[mine_f], fleft.at[mine_f], partner)
    f_start(13, fright.at[mine_f], fright.at[mine_f], partner)


    arrive[8].wait_recv()
    arrive[10].wait_recv()
    sent[18].start()
    arrive[17].wait_recv()
    multiply(far)
    arrive[9].wait_recv()
    arrive[11].wait_recv()
    sent[19].start()
    arrive[18].wait_recv()
    multiply(low2)
    arrive[12].wait_recv()
    arrive[13].wait_recv()
    sent[20].start()
    arrive[19].wait_recv()
    multiply(high2)
    theirs = pl.ds((1 - core) * (NX * NZH), NX * NZH)
    f_wait(12, fleft.at[theirs])
    f_wait(13, fright.at[theirs])
    for k in range(POP):
        c_, rest = divmod(k, NX * NZH)
        x_, zh_ = divmod(rest, NZH)
        first = (zh_ * (NX * NC) + x_ * NC + c_) * members
        for m in range(members):
            r = slice((k * members + m) * 4, (k * members + m) * 4 + 4)
            rank = jnp.full((4, share), ranks[first + m], jnp.int32).astype(jnp.float32)
            fitness = rank / (POP * members - 1) - 0.5
            wide_left[r, :] = fleft[k, m].astype(jnp.float32) * fitness
            wide_right[r, :] = fright[k, m].astype(jnp.float32)
    step_factor = math.sqrt(width) / (noise_scale * POP * members)
    turned = wide_left[...].T.astype(jnp.bfloat16)
    for n in range(0, outputs, 256):
        product = jnp.dot(turned, wide_right[:, n:n + 256].astype(jnp.bfloat16),
                          preferred_element_type=jnp.float32)
        step[:, n:n + 256] = (product * step_factor).astype(jnp.bfloat16)

    arrive[20].wait_recv()
    multiply(far2)

    for cp in t_loads:
        cp.wait()
    lanes = lax.broadcasted_iota(jnp.int32, (1, rows), 1)
    partial = []
    for m in range(members):
        running = jnp.zeros((1, rows), jnp.float32)
        for q in range(span // rows):
            r = slice(m * span + q * rows, m * span + (q + 1) * rows)
            part = jnp.zeros((rows, 128), jnp.float32)
            for g in range(0, outputs, 128):
                e = acc[r, g:g + 128] - tbuf[r, g:g + 128].astype(jnp.float32)
                part = part + e * e
            row = jnp.sum(part.T, axis=0, keepdims=True) / outputs
            position = shard * span + q * rows + lanes
            row = jnp.where(position < lengths[m], row, 0.0)
            losses[m:m + 1, q * rows:(q + 1) * rows] = row
            running = running + row
        partial.append(jnp.sum(running, axis=1, keepdims=True))
    which = lax.broadcasted_iota(jnp.int32, (8, 128), 0)
    mine[...] = jnp.where(which == 0, partial[0], partial[1])

    s_sent = []
    for d, peer in enumerate(shard_peers):
        cp = pltpu.make_async_remote_copy(
            src_ref=mine, dst_ref=sums.at[d], send_sem=send_s.at[d], recv_sem=recv_s.at[d],
            device_id=peer, device_id_type=MESH)
        cp.start()
        s_sent.append(cp)
    for i in range(21):
        sent[i].wait_send()
    for cp in f_sent:
        cp.wait_send()
    for cp in s_sent:
        cp.wait()
    whole = jnp.zeros((8, 128), jnp.float32)
    for s in range(SHARDS):
        term = mine[...]
        for d in range(SHARDS - 1):
            term = jnp.where(lax.rem(shard + SHARDS - d - 1, SHARDS) == s, sums[d], term)
        whole = whole + term
    for m in range(members):
        count = jnp.full((8, 128), lengths[m], jnp.int32).astype(jnp.float32)
        scores[m] = (whole / count)[m, 0]


def settle(losses_in, scores_in, step_in, losses, scores, step):
    losses[...] = losses_in[...]
    for m in range(scores.shape[0]):
        scores[m] = scores_in[m]
    step[...] = step_in[...]


def on_device(hidden, gain, weights, left, right, target, lengths, ranks):
    members, span, width = hidden.shape
    share, outputs = weights.shape
    rank = left.shape[1]
    tokens = members * span
    bf, f32 = jnp.bfloat16, jnp.float32
    hbm = pl.BlockSpec(memory_space=pl.ANY)
    vmem = pl.BlockSpec(memory_space=pltpu.VMEM)
    smem = pl.BlockSpec(memory_space=pltpu.SMEM)
    dma = pltpu.SemaphoreType.DMA
    results = pl.pallas_call(
        kernel,
        out_shape=(
            jax.ShapeDtypeStruct((members, span), f32),
            jax.ShapeDtypeStruct((members,), f32),
            jax.ShapeDtypeStruct((share, outputs), bf),
        ),
        in_specs=[hbm, vmem, hbm, hbm, hbm, vmem, vmem, hbm, smem, smem],
        out_specs=(vmem, smem, vmem),
        scratch_shapes=[
            pltpu.VMEM((tokens, width), bf),
            pltpu.VMEM((SHARDS, tokens, share), bf),
            pltpu.VMEM((SHARDS, share, outputs), bf),
            pltpu.VMEM((tokens, outputs), f32),
            pltpu.VMEM((tokens, outputs), bf),
            pltpu.VMEM((members, SHARDS, 16, share), bf),
            pltpu.VMEM((members, 16, outputs), bf),
            pltpu.VMEM((POP, members, rank, share), bf),
            pltpu.VMEM((POP, members, rank, outputs), bf),
            pltpu.VMEM((POP * members * rank, share), f32),
            pltpu.VMEM((POP * members * rank, outputs), f32),
            pltpu.VMEM((8, 128), f32),
            pltpu.VMEM((SHARDS - 1, 8, 128), f32),
            dma((tokens // 128 + 3 + members,)),
            dma((21,)), dma((21,)), dma((14,)), dma((14,)), dma((7,)), dma((7,)),
        ],
        compiler_params=pltpu.CompilerParams(
            collective_id=0, has_side_effects=True, vmem_limit_bytes=60 * 1024 * 1024),
    )(hidden, gain.reshape(1, width), weights, left, right, left, right, target, lengths, ranks)
    return tuple(pl.pallas_call(
        settle,
        out_shape=tuple(jax.ShapeDtypeStruct(r.shape, r.dtype) for r in results),
        in_specs=[vmem, smem, vmem],
        out_specs=(vmem, smem, vmem),
    )(*results))


def solution(mesh):
    placed = (
        P("pop", "shard", None),
        P(),
        P("shard", None),
        P("pop", None, None),
        P("pop", None, None),
        P("pop", "shard", None),
        P("pop"),
        P(),
    )
    return jax.shard_map(
        on_device,
        mesh=mesh,
        in_specs=placed,
        out_specs=(P("pop", "shard"), P("pop"), P("shard", None)),
        check_vma=False,
    )
```

```python
import math

import jax
import jax.numpy as jnp
from jax import lax
from jax.experimental import pallas as pl
from jax.experimental.pallas import tpu as pltpu
from jax.sharding import PartitionSpec as P

noise_scale = 0.1
epsilon = 1e-05
MESH = pl.DeviceIdType.MESH
NX, NY, NZH, NZL, NC = 4, 4, 4, 2, 2
SHARDS = NZL * NY
POP = NZH * NX * NC


def kernel(
    hidden, gain, weights, left, right, left_in, right_in, target, lengths, ranks,
    losses, scores, step,
    hbuf, nbuf, wbuf, acc, tbuf, abuf, bbuf, fleft, fright, wide_left, wide_right, mine, sums,
    load_sem, send_w, recv_w, send_f, recv_f, send_s, recv_s,
):
    members, span, width = hidden.shape
    share, outputs = weights.shape
    half, quarter = share // 2, share // 4
    pop, shard = lax.axis_index("pop"), lax.axis_index("shard")
    core = lax.rem(pop, NC)
    x = lax.rem(pop // NC, NX)
    zh = pop // (NC * NX)
    zl, y = shard // NY, lax.rem(shard, NY)

    def device(x_, zh_, core_, zl_, y_):
        return (zh_ * (NX * NC) + x_ * NC + core_, zl_ * NY + y_)

    up, down, across = lax.rem(y + 1, NY), lax.rem(y + 3, NY), lax.rem(y + 2, NY)
    other = 1 - zl
    partner = device(x, zh, 1 - core, zl, y)
    y_next, y_prev = device(x, zh, core, zl, up), device(x, zh, core, zl, down)
    z_next = device(x, lax.rem(zh + zl, NZH), core, other, y)
    z_prev = device(x, lax.rem(zh + NZH - other, NZH), core, other, y)
    z_pop = jnp.where(core == 0, z_next[0], z_prev[0])
    z_to = (z_pop, z_next[1])
    z_peers = [device(x, lax.rem(zh + d, NZH), core, zl, y) for d in (1, 2, 3)]
    x_peers = [device(lax.rem(x + d, NX), zh, core, zl, y) for d in (1, 2, 3)]
    shard_peers = [(pop, lax.rem(shard + d, SHARDS)) for d in range(1, SHARDS)]

    own, low_, high, far = zl * NY + y, zl * NY + down, zl * NY + up, zl * NY + across
    own2, low2, high2, far2 = (other * NY + v for v in (y, down, up, across))

    loads = []
    rows = 128
    chunks = members * span // rows
    for j in range(chunks):
        m, q = divmod(j, span // rows)
        loads.append(pltpu.make_async_copy(
            hidden.at[m, pl.ds(q * rows, rows)], hbuf.at[pl.ds(j * rows, rows)], load_sem.at[j]))
    own_load = pltpu.make_async_copy(weights, wbuf.at[own], load_sem.at[chunks])
    slot = core * (NX * NZH) + x * NZH + zh
    columns = pl.ds(pl.multiple_of(shard * share, share), share)
    fl_load = pltpu.make_async_copy(left.at[:, :, columns], fleft.at[slot], load_sem.at[chunks + 1])
    fr_load = pltpu.make_async_copy(right, fright.at[slot], load_sem.at[chunks + 2])
    t_loads = [pltpu.make_async_copy(target.at[m], tbuf.at[pl.ds(m * span, span)],
                                     load_sem.at[chunks + 3 + m]) for m in range(members)]
    for cp in loads + [own_load, fl_load, fr_load] + t_loads:
        cp.start()

    barrier = pltpu.get_barrier_semaphore()
    everyone = [partner, z_next, z_prev] + z_peers + x_peers + shard_peers
    for peer in everyone:
        pl.semaphore_signal(barrier, inc=1, device_id=peer, device_id_type=MESH)
    for m in range(members):
        pad = jnp.zeros((12, width), jnp.float32)
        a = jnp.concatenate([left_in[m].astype(jnp.float32), pad], axis=0).astype(jnp.bfloat16)
        for b in range(SHARDS):
            abuf[m, b] = a[:, b * share:(b + 1) * share]
        pad = jnp.zeros((12, outputs), jnp.float32)
        bbuf[m] = jnp.concatenate([right_in[m].astype(jnp.float32), pad], axis=0).astype(jnp.bfloat16)
    pl.semaphore_wait(barrier, len(everyone))

    def w_copy(i, src, dst, to):
        return pltpu.make_async_remote_copy(
            src_ref=src, dst_ref=dst, send_sem=send_w.at[i], recv_sem=recv_w.at[i],
            device_id=to, device_id_type=MESH)

    def f_copy(i, src, dst, to):
        return pltpu.make_async_remote_copy(
            src_ref=src, dst_ref=dst, send_sem=send_f.at[i], recv_sem=recv_f.at[i],
            device_id=to, device_id_type=MESH)

    def at(sub):
        return pl.ds(pl.multiple_of(core * half + sub * quarter, quarter), quarter)

    def piece(b, sub):
        return wbuf.at[b, at(sub)]

    def half_of(b, c):
        return wbuf.at[b, pl.ds(pl.multiple_of(c * half, half), half)]

    sent, arrive = {}, {}

    def plan(i, src, dst, landing, to):
        sent[i] = w_copy(i, src, dst, to)
        arrive[i] = w_copy(i, landing, landing, to)

    for i, sub in ((0, 0), (1, 1)):
        plan(i, weights.at[at(sub)], piece(own, sub), piece(low_, sub), y_next)
    plan(2, piece(low_, 0), piece(low_, 0), piece(far, 0), y_next)
    for i, sub in ((3, 1), (4, 0)):
        plan(i, weights.at[at(sub)], piece(own, sub), piece(high, sub), y_prev)
    plan(5, piece(high, 1), piece(high, 1), piece(far, 1), y_prev)
    for i, sub in ((6, 0), (7, 1)):
        plan(i, weights.at[at(sub)], piece(own, sub), piece(own2, sub), z_to)
    for i, b, b2, sub in ((8, low_, low2, 0), (9, high, high2, 1), (10, low_, low2, 1),
                          (11, high, high2, 0), (12, far, far2, 0), (13, far, far2, 1)):
        plan(i, piece(b, sub), piece(b, sub), piece(b2, sub), z_to)
    for i, b in ((14, low_), (15, high), (16, own2), (17, far), (18, low2), (19, high2), (20, far2)):
        plan(i, half_of(b, core), half_of(b, core), half_of(b, 1 - core), partner)

    f_sent = []

    def f_start(i, src, dst, to):
        cp = f_copy(i, src, dst, to)
        cp.start()
        f_sent.append(cp)

    for d in range(3):
        f_start(2 * d, left.at[:, :, columns], fleft.at[slot], z_peers[d])
        f_start(2 * d + 1, right, fright.at[slot], z_peers[d])
    for i in (0, 3, 6, 1, 4, 7):
        sent[i].start()

    tile = 16
    for j in range(chunks):
        loads[j].wait()

        def norm(t, carry, j=j):
            r = pl.ds(pl.multiple_of(j * rows + t * tile, tile), tile)
            total = jnp.zeros((tile, share), jnp.float32)
            for b in range(SHARDS):
                v = hbuf[r, b * share:(b + 1) * share].astype(jnp.float32)
                total = total + v * v
            inverse = lax.rsqrt(jnp.sum(total, axis=-1, keepdims=True) / width + epsilon)
            for b in range(SHARDS):
                cols = slice(b * share, (b + 1) * share)
                v = hbuf[r, cols].astype(jnp.float32)
                nbuf[b, r] = (v * inverse * gain[:, cols]).astype(jnp.bfloat16)
            return carry

        lax.fori_loop(0, rows // tile, norm, 0)

    arrive[0].wait_recv()
    sent[2].start()
    sent[8].start()
    arrive[3].wait_recv()
    sent[5].start()
    sent[9].start()

    def f_wait(i, dst):
        f_copy(i, dst, dst, partner).wait_recv()

    for m in range(members):
        r = pl.ds(m * span, span)
        low = jnp.zeros((span, 16), jnp.float32)
        for b in range(SHARDS):
            low = low + lax.dot_general(
                nbuf[b, r], abuf[m, b], (((1,), (1,)), ((), ())), preferred_element_type=jnp.float32)
        low = low.astype(jnp.bfloat16)
        for n in range(0, outputs, 256):
            acc[r, n:n + 256] = noise_scale * jnp.dot(
                low, bbuf[m, :, n:n + 256], preferred_element_type=jnp.float32)

    def multiply(b):
        def body(t, carry):
            c = pl.ds(pl.multiple_of(t * 256, 256), 256)
            acc[:, c] += jnp.dot(nbuf[b], wbuf[b, :, c], preferred_element_type=jnp.float32)
            return carry

        lax.fori_loop(0, outputs // 256, body, 0)

    own_load.wait()
    multiply(own)

    for d in range(3):
        back = core * (NX * NZH) + x * NZH + lax.rem(zh + NZH - d - 1, NZH)
        f_wait(2 * d, fleft.at[back])
        f_wait(2 * d + 1, fright.at[back])
    fl_load.wait()
    fr_load.wait()
    group = pl.ds(core * (NX * NZH) + x * NZH, NZH)
    for d in range(3):
        f_start(6 + 2 * d, fleft.at[group], fleft.at[group], x_peers[d])
        f_start(7 + 2 * d, fright.at[group], fright.at[group], x_peers[d])


    for i in (6, 7):
        arrive[i].wait_recv()
    sent[16].start()
    arrive[1].wait_recv()
    sent[10].start()
    sent[14].start()
    arrive[4].wait_recv()
    sent[11].start()
    sent[15].start()

    arrive[16].wait_recv()
    multiply(own2)
    arrive[14].wait_recv()
    multiply(low_)
    arrive[2].wait_recv()
    sent[12].start()
    arrive[5].wait_recv()
    sent[13].start()
    sent[17].start()
    arrive[15].wait_recv()
    multiply(high)

    for d in range(3):
        g = pl.ds(core * (NX * NZH) + lax.rem(x + NX - d - 1, NX) * NZH, NZH)
        f_wait(6 + 2 * d, fleft.at[g])
        f_wait(7 + 2 * d, fright.at[g])
    mine_f = pl.ds(core * (NX * NZH), NX * NZH)
    f_start(12, fleft.at[mine_f], fleft.at[mine_f], partner)
    f_start(13, fright.at[mine_f], fright.at[mine_f], partner)


    arrive[8].wait_recv()
    arrive[10].wait_recv()
    sent[18].start()
    arrive[17].wait_recv()
    multiply(far)
    arrive[9].wait_recv()
    arrive[11].wait_recv()
    sent[19].start()
    arrive[18].wait_recv()
    multiply(low2)
    theirs = pl.ds((1 - core) * (NX * NZH), NX * NZH)
    f_wait(12, fleft.at[theirs])
    f_wait(13, fright.at[theirs])
    for k in range(POP):
        c_, rest = divmod(k, NX * NZH)
        x_, zh_ = divmod(rest, NZH)
        first = (zh_ * (NX * NC) + x_ * NC + c_) * members
        for m in range(members):
            r = slice((k * members + m) * 4, (k * members + m) * 4 + 4)
            rank = jnp.full((4, share), ranks[first + m], jnp.int32).astype(jnp.float32)
            fitness = rank / (POP * members - 1) - 0.5
            wide_left[r, :] = fleft[k, m].astype(jnp.float32) * fitness
            wide_right[r, :] = fright[k, m].astype(jnp.float32)
    step_factor = math.sqrt(width) / (noise_scale * POP * members)
    turned = wide_left[...].T.astype(jnp.bfloat16)
    for n in range(0, outputs, 256):
        product = jnp.dot(turned, wide_right[:, n:n + 256].astype(jnp.bfloat16),
                          preferred_element_type=jnp.float32)
        step[:, n:n + 256] = (product * step_factor).astype(jnp.bfloat16)

    arrive[12].wait_recv()
    arrive[13].wait_recv()
    sent[20].start()
    arrive[19].wait_recv()
    multiply(high2)
    arrive[20].wait_recv()
    multiply(far2)

    for cp in t_loads:
        cp.wait()
    lanes = lax.broadcasted_iota(jnp.int32, (1, rows), 1)
    partial = []
    for m in range(members):
        running = jnp.zeros((1, rows), jnp.float32)
        for q in range(span // rows):
            r = slice(m * span + q * rows, m * span + (q + 1) * rows)
            part = jnp.zeros((rows, 128), jnp.float32)
            for g in range(0, outputs, 128):
                e = acc[r, g:g + 128] - tbuf[r, g:g + 128].astype(jnp.float32)
                part = part + e * e
            row = jnp.sum(part.T, axis=0, keepdims=True) / outputs
            position = shard * span + q * rows + lanes
            row = jnp.where(position < lengths[m], row, 0.0)
            losses[m:m + 1, q * rows:(q + 1) * rows] = row
            running = running + row
        partial.append(jnp.sum(running, axis=1, keepdims=True))
    which = lax.broadcasted_iota(jnp.int32, (8, 128), 0)
    mine[...] = jnp.where(which == 0, partial[0], partial[1])

    s_sent = []
    for d, peer in enumerate(shard_peers):
        cp = pltpu.make_async_remote_copy(
            src_ref=mine, dst_ref=sums.at[d], send_sem=send_s.at[d], recv_sem=recv_s.at[d],
            device_id=peer, device_id_type=MESH)
        cp.start()
        s_sent.append(cp)
    for i in range(21):
        sent[i].wait_send()
    for cp in f_sent:
        cp.wait_send()
    for cp in s_sent:
        cp.wait()
    whole = jnp.zeros((8, 128), jnp.float32)
    for s in range(SHARDS):
        term = mine[...]
        for d in range(SHARDS - 1):
            term = jnp.where(lax.rem(shard + SHARDS - d - 1, SHARDS) == s, sums[d], term)
        whole = whole + term
    for m in range(members):
        count = jnp.full((8, 128), lengths[m], jnp.int32).astype(jnp.float32)
        scores[m] = (whole / count)[m, 0]


def settle(losses_in, scores_in, step_in, losses, scores, step):
    losses[...] = losses_in[...]
    for m in range(scores.shape[0]):
        scores[m] = scores_in[m]
    step[...] = step_in[...]


def on_device(hidden, gain, weights, left, right, target, lengths, ranks):
    members, span, width = hidden.shape
    share, outputs = weights.shape
    rank = left.shape[1]
    tokens = members * span
    bf, f32 = jnp.bfloat16, jnp.float32
    hbm = pl.BlockSpec(memory_space=pl.ANY)
    vmem = pl.BlockSpec(memory_space=pltpu.VMEM)
    smem = pl.BlockSpec(memory_space=pltpu.SMEM)
    dma = pltpu.SemaphoreType.DMA
    results = pl.pallas_call(
        kernel,
        out_shape=(
            jax.ShapeDtypeStruct((members, span), f32),
            jax.ShapeDtypeStruct((members,), f32),
            jax.ShapeDtypeStruct((share, outputs), bf),
        ),
        in_specs=[hbm, vmem, hbm, hbm, hbm, vmem, vmem, hbm, smem, smem],
        out_specs=(vmem, smem, vmem),
        scratch_shapes=[
            pltpu.VMEM((tokens, width), bf),
            pltpu.VMEM((SHARDS, tokens, share), bf),
            pltpu.VMEM((SHARDS, share, outputs), bf),
            pltpu.VMEM((tokens, outputs), f32),
            pltpu.VMEM((tokens, outputs), bf),
            pltpu.VMEM((members, SHARDS, 16, share), bf),
            pltpu.VMEM((members, 16, outputs), bf),
            pltpu.VMEM((POP, members, rank, share), bf),
            pltpu.VMEM((POP, members, rank, outputs), bf),
            pltpu.VMEM((POP * members * rank, share), f32),
            pltpu.VMEM((POP * members * rank, outputs), f32),
            pltpu.VMEM((8, 128), f32),
            pltpu.VMEM((SHARDS - 1, 8, 128), f32),
            dma((tokens // 128 + 3 + members,)),
            dma((21,)), dma((21,)), dma((14,)), dma((14,)), dma((7,)), dma((7,)),
        ],
        compiler_params=pltpu.CompilerParams(
            collective_id=0, has_side_effects=True, vmem_limit_bytes=60 * 1024 * 1024),
    )(hidden, gain.reshape(1, width), weights, left, right, left, right, target, lengths, ranks)
    return tuple(pl.pallas_call(
        settle,
        out_shape=tuple(jax.ShapeDtypeStruct(r.shape, r.dtype) for r in results),
        in_specs=[vmem, smem, vmem],
        out_specs=(vmem, smem, vmem),
    )(*results))


def solution(mesh):
    placed = (
        P("pop", "shard", None),
        P(),
        P("shard", None),
        P("pop", None, None),
        P("pop", None, None),
        P("pop", "shard", None),
        P("pop"),
        P(),
    )
    return jax.shard_map(
        on_device,
        mesh=mesh,
        in_specs=placed,
        out_specs=(P("pop", "shard"), P("pop"), P("shard", None)),
        check_vma=False,
    )
```
